512 devices in a mesh: traj: 8 (over z), dom: 64 (over x, y, core).
Axes of the slice: x: 4, y: 8, z: 8, core: 2. Of those that a mesh axis runs over, the one named last changes fastest.
Arguments:
- node_lat: bfloat16 [8, 16384, 512], P('traj', 'dom'), may hold values from -6 to 6
- edge_lat: bfloat16 [8, 32768, 512], P('traj', 'dom'), may hold values from -6 to 6
- grad_edge: bfloat16 [8, 32768, 512], P('traj', 'dom'), may hold values from -6 to 6
- grad_agg: bfloat16 [8, 16384, 512], P('traj', 'dom'), may hold values from -6 to 6
- weight_edge: bfloat16 [512, 512], replicated, may hold values from -0.15625 to 0.15625
- weight_send: bfloat16 [512, 512], replicated, may hold values from -0.15625 to 0.15625
- weight_recv: bfloat16 [512, 512], replicated, may hold values from -0.15625 to 0.15625
- weight_out: bfloat16 [512, 512], replicated, may hold values from -0.25 to 0.25
- edge_src: int32 [32768], P('dom'), may hold values from 0 to 767
- edge_recv_block: int32 [256], P('dom'), may hold values from 0 to 1
- edge_recv_node: int32 [32768], P('dom'), may hold values from 0 to 127
- send_blocks: int32 [256], P('dom'), may hold values from 0 to 1
Outputs:
- agg: bfloat16 [8, 16384, 512], P('traj', 'dom')
- grad_edge_lat: bfloat16 [8, 32768, 512], P('traj', 'dom')
- grad_node_lat: bfloat16 [8, 16384, 512], P('traj', 'dom')
- weight_grads: float32 [4, 512, 512], P(None, 'dom')
The draws below stay inside these ranges and needn't reach their ends.
Inputs may be any that keep to these rules, and one draw needn't show every extreme that they name: edge_src // 128 is a slot below 6.
All inputs are finite; a program needn't handle non-finite values.
Results may differ from the reference program's by a relative error of at most 0.012.
Values may be sent and summed in bfloat16 or wider, within the bound.
A program may use at most 64 MiB of HBM per device.

```python
import jax
import jax.numpy as jnp
from jax import lax

D = 512
EB_DEV = 4
NB_DEV = 2
ROUNDS = 4
EDGES = 32768
NODES = 16384
EDGE_BLOCKS = 256
SEND_ROWS = 256
N_TRAJ = 8
N_DOM = 64


def plant(array, stream_key, low, high):
    longest = array.shape.index(max(array.shape))
    spots = []
    for shift in (0, 1):
        where = [jax.random.randint(jax.random.fold_in(stream_key, axis), (), 0, length) for axis, length in enumerate(array.shape)]
        where[longest] = (where[longest] + shift) % array.shape[longest]
        spots.append(tuple(where))
    return array.at[spots[0]].set(low).at[spots[1]].set(high)


def steps_of(rng, dims, cuts, low, high):
    def one(axis_at, shards_of):
        heights = jax.random.uniform(jax.random.fold_in(jax.random.fold_in(rng, 6), axis_at), (shards_of,), jnp.float32, low / len(cuts), high / len(cuts))
        return jnp.repeat(jnp.exp(heights), dims[axis_at] // shards_of).reshape((-1,) + (1,) * (len(dims) - axis_at - 1))

    loudness = one(*cuts[0])
    for cut in cuts[1:]:
        loudness = loudness * one(*cut)
    return loudness


def normal_values(stream_key, shape, width, limit, cuts=(), kind=jnp.bfloat16):
    gain = steps_of(stream_key, shape, cuts, -0.22, 0.18) if cuts else 1.0
    array = jax.random.normal(stream_key, shape, jnp.float32) * width * gain
    return jnp.minimum(jnp.maximum(array, -limit), limit).astype(kind)


def setup_inputs(seed: int = 0) -> dict:
    streams_of = jax.random.split(jax.random.key(seed), 13)
    node_lat = normal_values(streams_of[0], (N_TRAJ, NODES, D), 1.0, 6.0, ((0, 8), (1, 64)))
    edge_lat = normal_values(streams_of[1], (N_TRAJ, EDGES, D), 1.0, 6.0, ((0, 8), (1, 64)))
    grad_edge = normal_values(streams_of[2], (N_TRAJ, EDGES, D), 1.0, 6.0, ((0, 8), (1, 64)))
    grad_agg = normal_values(streams_of[3], (N_TRAJ, NODES, D), 1.0, 6.0, ((0, 8), (1, 64)))
    weight_edge = normal_values(streams_of[4], (D, D), (3 * D) ** -0.5, 0.15625)
    weight_send = normal_values(streams_of[5], (D, D), (3 * D) ** -0.5, 0.15625)
    weight_recv = normal_values(streams_of[6], (D, D), (3 * D) ** -0.5, 0.15625)
    weight_out = normal_values(streams_of[7], (D, D), D ** -0.5, 0.25)
    edge_src = plant(jax.random.randint(streams_of[8], (EDGES,), 0, (NB_DEV + ROUNDS) * 128), jax.random.fold_in(streams_of[8], 1), 0, ((NB_DEV + ROUNDS) * 128) - 1).astype(jnp.int32)
    edge_recv_block = plant(jax.random.randint(streams_of[9], (EDGE_BLOCKS,), 0, NB_DEV), jax.random.fold_in(streams_of[9], 1), 0, NB_DEV - 1).astype(jnp.int32)
    edge_recv_node = plant(jax.random.randint(streams_of[10], (EDGES,), 0, 128), jax.random.fold_in(streams_of[10], 1), 0, 127).astype(jnp.int32)
    send_blocks = plant(jax.random.randint(streams_of[11], (SEND_ROWS,), 0, NB_DEV), jax.random.fold_in(streams_of[11], 1), 0, NB_DEV - 1).astype(jnp.int32)
    return {"node_lat": node_lat, "edge_lat": edge_lat, "grad_edge": grad_edge, "grad_agg": grad_agg, "weight_edge": weight_edge, "weight_send": weight_send, "weight_recv": weight_recv, "weight_out": weight_out, "edge_src": edge_src, "edge_recv_block": edge_recv_block, "edge_recv_node": edge_recv_node, "send_blocks": send_blocks}


def dot_rows(former, latter):
    return lax.dot_general(former, latter, (((0,), (0,)), ((), ())), preferred_element_type=jnp.float32)

def dot_cols(former, latter):
    return lax.dot_general(former, latter, (((1,), (1,)), ((), ())), preferred_element_type=jnp.float32)

def silu_grad(preact):
    sigmoid_val = jax.nn.sigmoid(preact)
    return sigmoid_val * (1.0 + preact * (1.0 - sigmoid_val))

def indices(edge_src, edge_recv_block, edge_recv_node, send_blocks):
    devices = jnp.arange(N_DOM, dtype=jnp.int32)
    sent_blocks = send_blocks.reshape(N_DOM, ROUNDS)
    columns = [devices[:, None] * NB_DEV + jnp.arange(NB_DEV, dtype=jnp.int32)[None, :]]
    for section in range(ROUNDS):
        partner = jnp.bitwise_xor(devices, 1 << section)
        columns.append((partner * NB_DEV + sent_blocks[partner, section])[:, None])
    slot_table = jnp.concatenate(columns, axis=1).astype(jnp.int32)
    edge_owner = (jnp.arange(EDGES, dtype=jnp.int32) // (EB_DEV * 128)).astype(jnp.int32)
    sender = slot_table[edge_owner, edge_src // 128] * 128 + edge_src % 128
    block_ids = jnp.repeat(edge_recv_block, 128, total_repeat_length=EDGES)
    receiver = edge_owner * (NB_DEV * 128) + block_ids * 128 + edge_recv_node
    return (sender.astype(jnp.int32), receiver.astype(jnp.int32))

def reference(node_lat, edge_lat, grad_edge, grad_agg, weight_edge, weight_send, weight_recv, weight_out, edge_src, edge_recv_block, edge_recv_node, send_blocks):
    sender, receiver = indices(edge_src, edge_recv_block, edge_recv_node, send_blocks)
    weight_sum = jnp.zeros((4, D, D), jnp.float32)
    agg_list, edge_list, node_list = ([], [], [])
    for member in range(N_TRAJ):
        node_rows = node_lat[member]
        edge_rows = edge_lat[member]
        send_rows = node_rows[sender]
        recv_rows = node_rows[receiver]
        preact = jnp.dot(edge_rows, weight_edge, preferred_element_type=jnp.float32)
        preact = preact + jnp.dot(send_rows, weight_send, preferred_element_type=jnp.float32)
        preact = preact + jnp.dot(recv_rows, weight_recv, preferred_element_type=jnp.float32)
        hidden = jax.nn.silu(preact).astype(jnp.bfloat16)
        projected = jnp.dot(hidden, weight_out, preferred_element_type=jnp.float32)
        centered = projected - lax.optimization_barrier(jnp.mean(projected, axis=1, keepdims=True))
        inv_std = lax.rsqrt(lax.optimization_barrier(jnp.mean(centered * centered, axis=1, keepdims=True)) + 1e-05)
        normed = centered * inv_std
        message = normed.astype(jnp.bfloat16)
        agg = jax.ops.segment_sum(message.astype(jnp.float32), receiver, num_segments=NODES)
        grad_msg = grad_edge[member].astype(jnp.float32) + grad_agg[member][receiver].astype(jnp.float32)
        grad_proj = inv_std * (grad_msg - lax.optimization_barrier(jnp.mean(grad_msg, axis=1, keepdims=True)) - normed * lax.optimization_barrier(jnp.mean(grad_msg * normed, axis=1, keepdims=True)))
        grad_proj = grad_proj.astype(jnp.bfloat16)
        grad_preact = (dot_cols(grad_proj, weight_out) * silu_grad(preact)).astype(jnp.bfloat16)
        weight_sum = weight_sum + jnp.stack([dot_rows(edge_rows, grad_preact), dot_rows(send_rows, grad_preact), dot_rows(recv_rows, grad_preact), dot_rows(hidden, grad_proj)])
        grad_edges = grad_edge[member].astype(jnp.float32) + dot_cols(grad_preact, weight_edge)
        grad_nodes = jax.ops.segment_sum(dot_cols(grad_preact, weight_send), sender, num_segments=NODES)
        grad_nodes = grad_nodes + jax.ops.segment_sum(dot_cols(grad_preact, weight_recv), receiver, num_segments=NODES)
        agg_list.append(agg.astype(jnp.bfloat16))
        edge_list.append(grad_edges.astype(jnp.bfloat16))
        node_list.append(grad_nodes.astype(jnp.bfloat16))
    return (jnp.stack(agg_list), jnp.stack(edge_list), jnp.stack(node_list), weight_sum)
```

```python
import jax
import jax.numpy as jnp
from jax import lax
from jax.experimental import pallas as pl
from jax.experimental.pallas import tpu as pltpu
from jax.sharding import PartitionSpec as P

ROUNDS = 4
F32 = jnp.float32
BF16 = jnp.bfloat16
MESH = pl.DeviceIdType.MESH
CHUNKS = (("xz", 0, 80), ("zx", 80, 48))


def mm(a, b):
    return jnp.dot(a, b, preferred_element_type=F32)


def mm_tn(a, b):
    return lax.dot_general(a, b, (((0,), (0,)), ((), ())), preferred_element_type=F32)


def mm_nt(a, b):
    return lax.dot_general(a, b, (((1,), (1,)), ((), ())), preferred_element_type=F32)


def kernel(
    node_h, edge_h, ge_h, ga_h, we_h, ws_h, wr_h, wo_h, src_h, rblk_h, rnode_h, sblk_h,
    agg_o, gedge_o, gnode_o, wg_o,
    table, edge, ge, ga, we, ws, wr, wo, src, rnode, rblk, sblk,
    lent, oh, oht, rh, rht, pre, gmsg, srows, hid, msg, gproj, gpre, slot_out, slot_in,
    part, core_in, quart, x_in0, z_in0, mid0, x_in1, z_in1, mid1, sums, y_in, fin, gath,
    agg_v, gedge_v, gnode_v,
    ld, ex_s, ex_r, rt_s, rt_r, co_s, co_r, xs_s, xs_r, zs_s, zs_r, ys_s, ys_r, ag_s, ag_r, st,
):
    t = lax.axis_index("traj")
    d = lax.axis_index("dom")
    x, y, c = d // 16, (d // 2) % 8, d % 2

    def dom(xx, yy, cc):
        return xx * 16 + yy * 2 + cc

    partners = [(t, d + 1 - 2 * c)]
    for r in range(1, ROUNDS):
        h = 1 << (r - 1)
        partners.append((t, dom(x, y + h - 2 * h * ((y // h) % 2), c)))
    x_peer = [(t, dom((x + k) % 4, y, c)) for k in range(1, 4)]
    y_peer = [(t, dom(x, (y + k) % 8, c)) for k in range(1, 8)]
    z_peer = [((t + k) % 8, d) for k in range(1, 8)]
    g_peer = z_peer + [((t + k) % 8, dom(x, y, 1 - c)) for k in range(8)]

    loads = {}

    def load(i, s, dst):
        loads[i] = pltpu.make_async_copy(s, dst, ld.at[i])
        loads[i].start()

    load(0, node_h.at[0], table.at[0:256])
    load(1, sblk_h, sblk)
    load(2, src_h, src)
    load(3, rblk_h, rblk)
    load(4, rnode_h, rnode)
    load(5, edge_h.at[0], edge)
    load(6, we_h, we)
    load(7, wr_h, wr)
    load(8, ga_h.at[0], ga)
    load(9, ge_h.at[0], ge)
    load(10, ws_h, ws)
    load(11, wo_h, wo)

    bar = pltpu.get_barrier_semaphore()
    greet = [partners[0]] + y_peer + x_peer + g_peer[:7] + g_peer[8:]
    for dev in greet:
        pl.semaphore_signal(bar, inc=1, device_id=dev, device_id_type=MESH)

    def remote(s, dst, ss, rs, dev):
        cp = pltpu.make_async_remote_copy(
            src_ref=s, dst_ref=dst, send_sem=ss, recv_sem=rs, device_id=dev, device_id_type=MESH
        )
        cp.start()
        return cp

    loads[0].wait()
    loads[1].wait()
    for r in range(ROUNDS):
        pick = jnp.broadcast_to(sblk[:, r : r + 1], (128, 512)) == 0
        lent[r] = jnp.where(pick, table[0:128, :].astype(F32), table[128:256, :].astype(F32)).astype(BF16)
    pl.semaphore_wait(bar, len(greet))
    ex = {}
    for r in (3, 2, 1, 0):
        ex[r] = remote(
            lent.at[r], table.at[256 + 128 * r : 384 + 128 * r], ex_s.at[r], ex_r.at[r], partners[r]
        )

    for i in (2, 3, 4):
        loads[i].wait()
    slots = lax.broadcasted_iota(jnp.int32, (768, 512), 0)
    oht[...] = (slots == src[...]).astype(F32).astype(BF16)
    own = lax.broadcasted_iota(jnp.int32, (256, 128), 0)
    for j in range(4):
        hit = own == rnode[:, 128 * j : 128 * (j + 1)] + rblk[:, j : j + 1] * 128
        rht[:, 128 * j : 128 * (j + 1)] = hit.astype(F32).astype(BF16)
    oh[...] = oht[...].T
    rh[...] = rht[...].T
    for i in (5, 6, 7, 8, 9):
        loads[i].wait()
    for e in (0, 256):
        rows = slice(e, e + 256)
        rrows = mm(rh[rows, :], table[0:256, :]).astype(BF16)
        pre[rows, :] = mm(edge[rows, :], we[...]) + mm(rrows, wr[...])
        gmsg[rows, :] = ge[rows, :].astype(F32) + mm(rh[rows, :], ga[...])
    for i in (10, 11):
        loads[i].wait()

    for r in range(ROUNDS):
        ex[r].wait_recv()

    for e in (0, 256):
        rows = slice(e, e + 256)
        sr = mm(oh[rows, :], table[...]).astype(BF16)
        srows[rows, :] = sr
        p = pre[rows, :] + mm(sr, ws[...])
        sig = 1.0 / (1.0 + jnp.exp(-p))
        hv = (p * sig).astype(BF16)
        hid[rows, :] = hv
        dsilu = sig * (1.0 + p * (1.0 - sig))
        proj = mm(hv, wo[...])
        cen = proj - jnp.mean(proj, axis=1, keepdims=True)
        inv = lax.rsqrt(jnp.mean(cen * cen, axis=1, keepdims=True) + 1e-05)
        nrm = cen * inv
        msg[rows, :] = nrm.astype(BF16)
        g = gmsg[rows, :]
        gp = inv * (
            g - jnp.mean(g, axis=1, keepdims=True) - nrm * jnp.mean(g * nrm, axis=1, keepdims=True)
        )
        gp = gp.astype(BF16)
        gproj[rows, :] = gp
        gpre[rows, :] = (mm_nt(gp, wo[...]) * dsilu).astype(BF16)

    ret = {}
    for r in (3, 2, 1, 0):
        rows = slice(256 + 128 * r, 384 + 128 * r)
        slot_out[r] = mm(oht[rows, :], gpre[...]).astype(BF16)
        ret[r] = remote(slot_out.at[r], slot_in.at[r], rt_s.at[r], rt_r.at[r], partners[r])

    core = []
    for m in range(4):
        lhs = (edge, srows, None, hid)[m]
        rhs = (gpre, gpre, None, gproj)[m]
        if m == 2:
            rsum = mm(rht[...], gpre[...]).astype(BF16)
            gw = mm_tn(table[0:256, :], rsum)
        else:
            gw = mm_tn(lhs[...], rhs[...])
        gw = gw.astype(BF16)
        for xx in range(4):
            for b in range(4):
                part[b // 2, xx, 2 * m + b % 2] = gw[128 * xx : 128 * (xx + 1), 128 * b : 128 * (b + 1)]
        core.append(
            remote(
                part.at[1 - c, :, 2 * m : 2 * m + 2],
                core_in.at[:, 2 * m : 2 * m + 2],
                co_s.at[m],
                co_r.at[m],
                partners[0],
            )
        )
    for m in range(4):
        core[m].wait_recv()
        z2 = slice(2 * m, 2 * m + 2)
        quart[:, z2] = (part[c, :, z2].astype(F32) + core_in[:, z2].astype(F32)).astype(BF16)

    bufs = ((x_in0, z_in0, mid0), (x_in1, z_in1, mid1))
    first, second = [], []
    for i, (order, lo, n) in enumerate(CHUNKS):
        xi, zi, _ = bufs[i]
        rs = slice(lo, lo + n)
        sent = []
        if order == "xz":
            for k in (2, 1, 3):
                sent.append(
                    remote(
                        quart.at[(x + k) % 4, :, rs], xi.at[k - 1],
                        xs_s.at[i, k - 1], xs_r.at[i, k - 1], x_peer[k - 1],
                    )
                )
        else:
            for k in (4, 3, 5, 2, 6, 1, 7):
                sent.append(
                    remote(
                        quart.at[:, (t + k) % 8, rs], zi.at[k - 1],
                        zs_s.at[i, k - 1], zs_r.at[i, k - 1], z_peer[k - 1],
                    )
                )
        first.append(sent)

    agg_v[...] = mm(rht[...], msg[...]).astype(BF16)
    out0 = pltpu.make_async_copy(agg_v, agg_o.at[0], st.at[0])
    out0.start()
    for e in (0, 256):
        rows = slice(e, e + 256)
        gedge_v[rows, :] = (ge[rows, :].astype(F32) + mm_nt(gpre[rows, :], we[...])).astype(BF16)
    out1 = pltpu.make_async_copy(gedge_v, gedge_o.at[0], st.at[1])
    out1.start()
    own_sum = [mm(oht[128 * b : 128 * (b + 1), :], gpre[...]) for b in range(2)]
    gn_recv = mm_nt(rsum, wr[...])

    for i, (order, lo, n) in enumerate(CHUNKS):
        xi, zi, mid = bufs[i]
        rs = slice(lo, lo + n)
        for cp in first[i]:
            cp.wait_recv()
        sent = []
        if order == "xz":
            acc = quart[x, :, rs].astype(F32)
            for k in range(3):
                acc = acc + xi[k].astype(F32)
            mid[...] = acc.astype(BF16)
            for k in (4, 3, 5, 2, 6, 1, 7):
                sent.append(
                    remote(
                        mid.at[(t + k) % 8], zi.at[k - 1],
                        zs_s.at[i, k - 1], zs_r.at[i, k - 1], z_peer[k - 1],
                    )
                )
        else:
            acc = quart[:, t, rs].astype(F32)
            for k in range(7):
                acc = acc + zi[k].astype(F32)
            mid[...] = acc.astype(BF16)
            for k in (2, 1, 3):
                sent.append(
                    remote(
                        mid.at[(x + k) % 4], xi.at[k - 1],
                        xs_s.at[i, k - 1], xs_r.at[i, k - 1], x_peer[k - 1],
                    )
                )
        second.append(sent)

    for r in range(ROUNDS):
        ret[r].wait_recv()
        v = slot_in[r].astype(F32)
        for b in range(2):
            own_sum[b] = own_sum[b] + v * (sblk[:, r : r + 1] == b).astype(F32)
    for b in range(2):
        rows = slice(128 * b, 128 * (b + 1))
        gn = gn_recv[rows, :] + mm_nt(own_sum[b].astype(BF16), ws[...])
        gnode_v[rows, :] = gn.astype(BF16)
    out2 = pltpu.make_async_copy(gnode_v, gnode_o.at[0], st.at[2])
    out2.start()

    for i, (order, lo, n) in enumerate(CHUNKS):
        xi, zi, mid = bufs[i]
        for cp in second[i]:
            cp.wait_recv()
        if order == "xz":
            acc = mid[t].astype(F32)
            for k in range(7):
                acc = acc + zi[k].astype(F32)
        else:
            acc = mid[x].astype(F32)
            for k in range(3):
                acc = acc + xi[k].astype(F32)
        for j in range(n // 16):
            sums[lo // 16 + j] = acc[16 * j : 16 * (j + 1), :].astype(BF16)

    ysent = []
    for k in (4, 3, 5, 2, 6, 1, 7):
        ysent.append(
            remote(sums.at[(y + k) % 8], y_in.at[k - 1], ys_s.at[k - 1], ys_r.at[k - 1], y_peer[k - 1])
        )
    for cp in ysent:
        cp.wait_recv()
    acc = sums[y].astype(F32)
    for k in range(7):
        acc = acc + y_in[k].astype(F32)
    fin[0] = acc[0:8, :]
    fin[1] = acc[8:16, :]
    slot = (t // 2, 2 * c + t % 2)
    gsent = []
    for i, dev in enumerate(g_peer):
        half = c if i < 7 else 1 - c
        gsent.append(remote(fin.at[half], gath.at[slot[0], slot[1]], ag_s.at[i], ag_r.at[i], dev))
    mine = pltpu.make_async_copy(fin.at[c], gath.at[slot[0], slot[1]], st.at[3])
    mine.start()
    mine.wait()
    for cp in gsent:
        cp.wait_recv()
    for b in range(4):
        wg_o[:, :, 128 * b : 128 * (b + 1)] = gath[:, b]

    for r in range(ROUNDS):
        ex[r].wait_send()
        ret[r].wait_send()
    for cp in core + first[0] + first[1] + second[0] + second[1] + ysent + gsent:
        cp.wait_send()
    out0.wait()
    out1.wait()
    out2.wait()


def per_device(
    node_lat, edge_lat, grad_edge, grad_agg, weight_edge, weight_send, weight_recv, weight_out,
    edge_src, edge_recv_block, edge_recv_node, send_blocks,
):
    vm, dma = pltpu.VMEM, pltpu.SemaphoreType.DMA
    big = (512, 512)
    scratch = [
        vm((768, 512), BF16), vm(big, BF16), vm(big, BF16), vm((256, 512), BF16),
        vm(big, BF16), vm(big, BF16), vm(big, BF16), vm(big, BF16),
        vm((1, 512), jnp.int32), vm((1, 512), jnp.int32),
        vm((1, 4), jnp.int32), vm((1, 4), jnp.int32),
        vm((4, 128, 512), BF16), vm((512, 768), BF16), vm((768, 512), BF16),
        vm((512, 256), BF16), vm((256, 512), BF16),
        vm(big, F32), vm(big, F32),
        vm(big, BF16), vm(big, BF16), vm(big, BF16), vm(big, BF16), vm(big, BF16),
        vm((4, 128, 512), BF16), vm((4, 128, 512), BF16),
        vm((2, 4, 8, 128, 128), BF16), vm((4, 8, 128, 128), BF16), vm((4, 8, 128, 128), BF16),
    ]
    for order, _, n in CHUNKS:
        if order == "xz":
            scratch += [vm((3, 8, n, 128), BF16), vm((7, n, 128), BF16), vm((8, n, 128), BF16)]
        else:
            scratch += [vm((3, n, 128), BF16), vm((7, 4, n, 128), BF16), vm((4, n, 128), BF16)]
    scratch += [
        vm((8, 16, 128), BF16), vm((7, 16, 128), BF16), vm((2, 8, 128), F32), vm((4, 4, 8, 128), F32),
        vm((256, 512), BF16), vm(big, BF16), vm((256, 512), BF16),
        dma((12,)), dma((4,)), dma((4,)), dma((4,)), dma((4,)), dma((4,)), dma((4,)),
        dma((2, 3)), dma((2, 3)), dma((2, 7)), dma((2, 7)), dma((7,)), dma((7,)),
        dma((15,)), dma((15,)), dma((4,)),
    ]
    hbm = pl.BlockSpec(memory_space=pl.ANY)
    return pl.pallas_call(
        kernel,
        out_shape=(
            jax.ShapeDtypeStruct((1, 256, 512), BF16),
            jax.ShapeDtypeStruct((1, 512, 512), BF16),
            jax.ShapeDtypeStruct((1, 256, 512), BF16),
            jax.ShapeDtypeStruct((4, 8, 512), F32),
        ),
        in_specs=[hbm] * 12,
        out_specs=(hbm, hbm, hbm, pl.BlockSpec(memory_space=pltpu.VMEM)),
        scratch_shapes=scratch,
        compiler_params=pltpu.CompilerParams(
            collective_id=0, has_side_effects=True, vmem_limit_bytes=56 << 20
        ),
        name="edge_update_backward",
    )(
        node_lat, edge_lat, grad_edge, grad_agg, weight_edge, weight_send, weight_recv, weight_out,
        edge_src.reshape(1, 512), edge_recv_block.reshape(1, 4),
        edge_recv_node.reshape(1, 512), send_blocks.reshape(1, 4),
    )


def solution(mesh):
    lat = P("traj", "dom", None)
    return jax.shard_map(
        per_device,
        mesh=mesh,
        in_specs=(lat,) * 4 + (P(),) * 4 + (P("dom"),) * 4,
        out_specs=(lat, lat, lat, P(None, "dom", None)),
        check_vma=False,
    )
```

```python
import jax
import jax.numpy as jnp
from jax import lax
from jax.experimental import pallas as pl
from jax.experimental.pallas import tpu as pltpu
from jax.sharding import PartitionSpec as P

ROUNDS = 4
F32 = jnp.float32
BF16 = jnp.bfloat16
MESH = pl.DeviceIdType.MESH
CHUNKS = (("xz", 0, 32), ("zx", 48, 16), ("xz", 32, 16))


def mm(a, b):
    return jnp.dot(a, b, preferred_element_type=F32)


def mm_tn(a, b):
    return lax.dot_general(a, b, (((0,), (0,)), ((), ())), preferred_element_type=F32)


def mm_nt(a, b):
    return lax.dot_general(a, b, (((1,), (1,)), ((), ())), preferred_element_type=F32)


def kernel(
    node_h, edge_h, ge_h, ga_h, we_h, ws_h, wr_h, wo_h, src_h, rblk_h, rnode_h, sblk_h,
    agg_o, gedge_o, gnode_o, wg_o,
    table, edge, ge, ga, we, ws, wr, wo, src, rnode, rblk, sblk,
    lent, oh, oht, rh, rht, pre, gmsg, srows, hid, msg, gproj, gpre, slot_out, slot_in,
    rsum, part, core_in, quart, x_in0, z_in0, mid0, x_in1, z_in1, mid1, x_in2, z_in2, mid2, sums, y_in, fin, gath,
    agg_v, gedge_v, gnode_v,
    ld, ex_s, ex_r, rt_s, rt_r, co_s, co_r, xs_s, xs_r, zs_s, zs_r, ys_s, ys_r, ag_s, ag_r, st,
):
    t = lax.axis_index("traj")
    d = lax.axis_index("dom")
    x, y, c = d // 16, (d // 2) % 8, d % 2

    def dom(xx, yy, cc):
        return xx * 16 + yy * 2 + cc

    partners = [(t, d + 1 - 2 * c)]
    for r in range(1, ROUNDS):
        h = 1 << (r - 1)
        partners.append((t, dom(x, y + h - 2 * h * ((y // h) % 2), c)))
    x_peer = [(t, dom((x + k) % 4, y, c)) for k in range(1, 4)]
    y_peer = [(t, dom(x, (y + k) % 8, c)) for k in range(1, 8)]
    z_peer = [((t + k) % 8, d) for k in range(1, 8)]

    loads, started, taken = {}, [], set()

    def load(i, s, dst):
        loads[i] = pltpu.make_async_copy(s, dst, ld.at[i])
        loads[i].start()

    load(0, node_h.at[0], table.at[0:256])
    load(1, sblk_h, sblk)
    load(2, src_h, src)
    load(3, rblk_h, rblk)
    load(4, rnode_h, rnode)
    load(5, edge_h.at[0], edge)
    load(6, we_h, we)
    load(7, wr_h, wr)
    load(8, ga_h.at[0], ga)
    load(9, ge_h.at[0], ge)
    load(10, ws_h, ws)
    load(11, wo_h, wo)

    bar = pltpu.get_barrier_semaphore()
    greet = [partners[0]] + y_peer + x_peer + z_peer
    for dev in greet:
        pl.semaphore_signal(bar, inc=1, device_id=dev, device_id_type=MESH)

    def remote(s, dst, ss, rs, dev):
        cp = pltpu.make_async_remote_copy(
            src_ref=s, dst_ref=dst, send_sem=ss, recv_sem=rs, device_id=dev, device_id_type=MESH
        )
        cp.start()
        started.append(cp)
        return cp

    def take(cp):
        cp.wait_recv()
        taken.add(id(cp))

    loads[0].wait()
    loads[1].wait()
    for r in range(ROUNDS):
        pick = jnp.broadcast_to(sblk[:, r : r + 1], (128, 512)) == 0
        lent[r] = jnp.where(pick, table[0:128, :].astype(F32), table[128:256, :].astype(F32)).astype(BF16)
    pl.semaphore_wait(bar, len(greet))
    ex = {}
    for r in (3, 2, 1, 0):
        ex[r] = remote(
            lent.at[r], table.at[256 + 128 * r : 384 + 128 * r], ex_s.at[r], ex_r.at[r], partners[r]
        )

    for i in (2, 3, 4):
        loads[i].wait()
    slots = lax.broadcasted_iota(jnp.int32, (768, 512), 0)
    oht[...] = (slots == src[...]).astype(F32).astype(BF16)
    own = lax.broadcasted_iota(jnp.int32, (256, 128), 0)
    for j in range(4):
        hit = own == rnode[:, 128 * j : 128 * (j + 1)] + rblk[:, j : j + 1] * 128
        rht[:, 128 * j : 128 * (j + 1)] = hit.astype(F32).astype(BF16)
    oh[...] = oht[...].T
    rh[...] = rht[...].T
    for i in (5, 6, 7, 8, 9):
        loads[i].wait()
    for e in (0, 256):
        rows = slice(e, e + 256)
        rrows = mm(rh[rows, :], table[0:256, :]).astype(BF16)
        pre[rows, :] = mm(edge[rows, :], we[...]) + mm(rrows, wr[...])
        gmsg[rows, :] = ge[rows, :].astype(F32) + mm(rh[rows, :], ga[...])
    for i in (10, 11):
        loads[i].wait()

    for r in range(ROUNDS):
        take(ex[r])

    for e in (0, 256):
        rows = slice(e, e + 256)
        sr = mm(oh[rows, :], table[...]).astype(BF16)
        srows[rows, :] = sr
        p = pre[rows, :] + mm(sr, ws[...])
        sig = 1.0 / (1.0 + jnp.exp(-p))
        hv = (p * sig).astype(BF16)
        hid[rows, :] = hv
        dsilu = sig * (1.0 + p * (1.0 - sig))
        proj = mm(hv, wo[...])
        cen = proj - jnp.mean(proj, axis=1, keepdims=True)
        inv = lax.rsqrt(jnp.mean(cen * cen, axis=1, keepdims=True) + 1e-05)
        nrm = cen * inv
        msg[rows, :] = nrm.astype(BF16)
        g = gmsg[rows, :]
        gp = inv * (
            g - jnp.mean(g, axis=1, keepdims=True) - nrm * jnp.mean(g * nrm, axis=1, keepdims=True)
        )
        gp = gp.astype(BF16)
        gproj[rows, :] = gp
        gpre[rows, :] = (mm_nt(gp, wo[...]) * dsilu).astype(BF16)

    core, ret = [], {}
    bufs = ((x_in0, z_in0, mid0), (x_in1, z_in1, mid1), (x_in2, z_in2, mid2))
    first = [[] for _ in CHUNKS]

    def grad(m):
        if m == 0:
            gw = mm_tn(edge[...], gpre[...])
        elif m == 1:
            gw = mm_tn(srows[...], gpre[...])
        elif m == 2:
            gw = mm_tn(table[0:256, :], rsum[...])
        else:
            gw = mm_tn(hid[...], gproj[...])
        gw = gw.reshape(4, 8, 2, 8, 512)
        for xx in range(4):
            for cc in range(2):
                v = gw[xx, :, cc].reshape(64, 512).astype(BF16)
                part[cc, xx, 2 * m] = v[:, 0:256]
                part[cc, xx, 2 * m + 1] = v[:, 256:512]
        core.append(
            remote(
                part.at[1 - c, :, 2 * m : 2 * m + 2],
                core_in.at[:, 2 * m : 2 * m + 2],
                co_s.at[m],
                co_r.at[m],
                partners[0],
            )
        )

    def merge(m):
        take(core[m])
        z2 = slice(2 * m, 2 * m + 2)
        quart[:, z2] = (part[c, :, z2].astype(F32) + core_in[:, z2].astype(F32)).astype(BF16)

    def send_x(i, g):
        _, lo, n = CHUNKS[i]
        zs = slice(4 * g, 4 * g + 4)
        for k in (2, 1, 3):
            first[i].append(
                remote(
                    quart.at[(x + k) % 4, zs, lo : lo + n], bufs[i][0].at[k - 1, zs],
                    xs_s.at[i, g, k - 1], xs_r.at[i, g, k - 1], x_peer[k - 1],
                )
            )

    def send_z(i):
        _, lo, n = CHUNKS[i]
        for k in (4, 3, 5, 2, 6, 1, 7):
            first[i].append(
                remote(
                    quart.at[:, (t + k) % 8, lo : lo + n], bufs[i][1].at[k - 1],
                    zs_s.at[i, k - 1], zs_r.at[i, k - 1], z_peer[k - 1],
                )
            )

    grad(0)
    grad(1)
    rsum[...] = mm(rht[...], gpre[...]).astype(BF16)
    grad(2)
    merge(0)
    merge(1)
    send_x(0, 0)
    grad(3)
    for r in (3, 2, 1, 0):
        rows = slice(256 + 128 * r, 384 + 128 * r)
        slot_out[r] = mm(oht[rows, :], gpre[...]).astype(BF16)
        ret[r] = remote(slot_out.at[r], slot_in.at[r], rt_s.at[r], rt_r.at[r], partners[r])
    merge(2)
    merge(3)
    send_z(1)
    send_x(0, 1)
    send_x(2, 0)
    send_x(2, 1)

    agg_v[...] = mm(rht[...], msg[...]).astype(BF16)
    out0 = pltpu.make_async_copy(agg_v, agg_o.at[0], st.at[0])
    out0.start()
    for e in (0, 256):
        rows = slice(e, e + 256)
        gedge_v[rows, :] = (ge[rows, :].astype(F32) + mm_nt(gpre[rows, :], we[...])).astype(BF16)
    out1 = pltpu.make_async_copy(gedge_v, gedge_o.at[0], st.at[1])
    out1.start()
    own_sum = [mm(oht[128 * b : 128 * (b + 1), :], gpre[...]) for b in range(2)]
    gn_recv = mm_nt(rsum[...], wr[...])

    second = []
    for i, (order, lo, n) in enumerate(CHUNKS):
        xi, zi, mid = bufs[i]
        rs = slice(lo, lo + n)
        for cp in first[i]:
            take(cp)
        sent = []
        if order == "xz":
            acc = quart[x, :, rs].astype(F32)
            for k in range(3):
                acc = acc + xi[k].astype(F32)
            mid[...] = acc.astype(BF16)
            for k in (4, 3, 5, 2, 6, 1, 7):
                sent.append(
                    remote(
                        mid.at[(t + k) % 8], zi.at[k - 1],
                        zs_s.at[i, k - 1], zs_r.at[i, k - 1], z_peer[k - 1],
                    )
                )
        else:
            acc = quart[:, t, rs].astype(F32)
            for k in range(7):
                acc = acc + zi[k].astype(F32)
            mid[...] = acc.astype(BF16)
            for k in (2, 1, 3):
                sent.append(
                    remote(
                        mid.at[(x + k) % 4], xi.at[k - 1],
                        xs_s.at[i, 0, k - 1], xs_r.at[i, 0, k - 1], x_peer[k - 1],
                    )
                )
        second.append(sent)

    for i, (order, lo, n) in enumerate(CHUNKS):
        xi, zi, mid = bufs[i]
        for cp in second[i]:
            take(cp)
        if order == "xz":
            acc = mid[t].astype(F32)
            for k in range(7):
                acc = acc + zi[k].astype(F32)
        else:
            acc = mid[x].astype(F32)
            for k in range(3):
                acc = acc + xi[k].astype(F32)
        for j in range(n // 8):
            sums[lo // 8 + j] = acc[8 * j : 8 * (j + 1), :]

    ysent = []
    for k in (4, 3, 5, 2, 6, 1, 7):
        ysent.append(
            remote(sums.at[(y + k) % 8], y_in.at[k - 1], ys_s.at[k - 1], ys_r.at[k - 1], y_peer[k - 1])
        )

    for r in range(ROUNDS):
        take(ret[r])
        v = slot_in[r].astype(F32)
        for b in range(2):
            own_sum[b] = own_sum[b] + v * (sblk[:, r : r + 1] == b).astype(F32)
    for b in range(2):
        rows = slice(128 * b, 128 * (b + 1))
        gn = gn_recv[rows, :] + mm_nt(own_sum[b].astype(BF16), ws[...])
        gnode_v[rows, :] = gn.astype(BF16)
    out2 = pltpu.make_async_copy(gnode_v, gnode_o.at[0], st.at[2])
    out2.start()

    for cp in ysent:
        take(cp)
    acc = sums[y]
    for k in range(7):
        acc = acc + y_in[k]
    fin[...] = acc
    gsent = []
    for k in (4, 3, 5, 2, 6, 1, 7):
        gsent.append(remote(fin, gath.at[t], ag_s.at[k - 1], ag_r.at[k - 1], z_peer[k - 1]))
    gath[t] = acc
    for cp in gsent:
        take(cp)
    for m in range(4):
        for b in range(2):
            wg_o[m, :, 256 * b : 256 * (b + 1)] = gath[2 * m + b]

    for cp in started:
        cp.wait_send()
    out0.wait()
    out1.wait()
    out2.wait()


def place(*refs):
    copies = [pltpu.make_async_copy(refs[i], refs[i + 4], refs[8].at[i]) for i in range(4)]
    for cp in copies:
        cp.start()
    for cp in copies:
        cp.wait()


def per_device(
    node_lat, edge_lat, grad_edge, grad_agg, weight_edge, weight_send, weight_recv, weight_out,
    edge_src, edge_recv_block, edge_recv_node, send_blocks,
):
    vm, dma = pltpu.VMEM, pltpu.SemaphoreType.DMA
    big = (512, 512)
    scratch = [
        vm((768, 512), BF16), vm(big, BF16), vm(big, BF16), vm((256, 512), BF16),
        vm(big, BF16), vm(big, BF16), vm(big, BF16), vm(big, BF16),
        vm((1, 512), jnp.int32), vm((1, 512), jnp.int32),
        vm((1, 4), jnp.int32), vm((1, 4), jnp.int32),
        vm((4, 128, 512), BF16), vm((512, 768), BF16), vm((768, 512), BF16),
        vm((512, 256), BF16), vm((256, 512), BF16),
        vm(big, F32), vm(big, F32),
        vm(big, BF16), vm(big, BF16), vm(big, BF16), vm(big, BF16), vm(big, BF16),
        vm((4, 128, 512), BF16), vm((4, 128, 512), BF16),
        vm((256, 512), BF16),
        vm((2, 4, 8, 64, 256), BF16), vm((4, 8, 64, 256), BF16), vm((4, 8, 64, 256), BF16),
    ]
    for order, _, n in CHUNKS:
        if order == "xz":
            scratch += [vm((3, 8, n, 256), BF16), vm((7, n, 256), BF16), vm((8, n, 256), BF16)]
        else:
            scratch += [vm((3, n, 256), BF16), vm((7, 4, n, 256), BF16), vm((4, n, 256), BF16)]
    scratch += [
        vm((8, 8, 256), F32), vm((7, 8, 256), F32), vm((8, 256), F32), vm((8, 8, 256), F32),
        vm((256, 512), BF16), vm(big, BF16), vm((256, 512), BF16),
        dma((12,)), dma((4,)), dma((4,)), dma((4,)), dma((4,)), dma((4,)), dma((4,)),
        dma((3, 2, 3)), dma((3, 2, 3)), dma((3, 7)), dma((3, 7)), dma((7,)), dma((7,)),
        dma((7,)), dma((7,)), dma((3,)),
    ]
    hbm = pl.BlockSpec(memory_space=pl.ANY)
    results = pl.pallas_call(
        kernel,
        out_shape=(
            jax.ShapeDtypeStruct((1, 256, 512), BF16),
            jax.ShapeDtypeStruct((1, 512, 512), BF16),
            jax.ShapeDtypeStruct((1, 256, 512), BF16),
            jax.ShapeDtypeStruct((4, 8, 512), F32),
        ),
        in_specs=[hbm] * 12,
        out_specs=(hbm, hbm, hbm, pl.BlockSpec(memory_space=pltpu.VMEM)),
        scratch_shapes=scratch,
        compiler_params=pltpu.CompilerParams(
            collective_id=0, has_side_effects=True, vmem_limit_bytes=56 << 20
        ),
        name="edge_update_backward",
    )(
        node_lat, edge_lat, grad_edge, grad_agg, weight_edge, weight_send, weight_recv, weight_out,
        edge_src.reshape(1, 512), edge_recv_block.reshape(1, 4),
        edge_recv_node.reshape(1, 512), send_blocks.reshape(1, 4),
    )
    return pl.pallas_call(
        place,
        out_shape=tuple(jax.ShapeDtypeStruct(r.shape, r.dtype) for r in results),
        in_specs=[hbm] * 4,
        out_specs=(hbm,) * 4,
        scratch_shapes=[dma((4,))],
        name="place_results",
    )(*results)


def solution(mesh):
    lat = P("traj", "dom", None)
    return jax.shard_map(
        per_device,
        mesh=mesh,
        in_specs=(lat,) * 4 + (P(),) * 4 + (P("dom"),) * 4,
        out_specs=(lat, lat, lat, P(None, "dom", None)),
        check_vma=False,
    )
```

```python
import jax
import jax.numpy as jnp
from jax import lax
from jax.experimental import pallas as pl
from jax.experimental.pallas import tpu as pltpu
from jax.sharding import PartitionSpec as P

ROUNDS = 4
F32 = jnp.float32
BF16 = jnp.bfloat16
MESH = pl.DeviceIdType.MESH
CHUNKS = (("xz", 0, 32), ("zx", 48, 16), ("xz", 32, 16))


def mm(a, b):
    return jnp.dot(a, b, preferred_element_type=F32)


def mm_tn(a, b):
    return lax.dot_general(a, b, (((0,), (0,)), ((), ())), preferred_element_type=F32)


def mm_nt(a, b):
    return lax.dot_general(a, b, (((1,), (1,)), ((), ())), preferred_element_type=F32)


def kernel(
    node_h, edge_h, ge_h, ga_h, we_h, ws_h, wr_h, wo_h, src_h, rblk_h, rnode_h, sblk_h,
    agg_o, gedge_o, gnode_o, wg_o,
    table, edge, ge, ga, we, ws, wr, wo, src, rnode, rblk, sblk,
    lent, oh, oht, rh, rht, pre, gmsg, srows, hid, msg, gproj, gpre, slot_out, slot_in,
    rsum, part, core_in, quart, x_in0, z_in0, mid0, x_in1, z_in1, mid1, x_in2, z_in2, mid2, sums, y_in, fin, gath,
    ld, ex_s, ex_r, rt_s, rt_r, co_s, co_r, xs_s, xs_r, zs_s, zs_r, ys_s, ys_r, ag_s, ag_r,
):
    t = lax.axis_index("traj")
    d = lax.axis_index("dom")
    x, y, c = d // 16, (d // 2) % 8, d % 2

    def dom(xx, yy, cc):
        return xx * 16 + yy * 2 + cc

    partners = [(t, d + 1 - 2 * c)]
    for r in range(1, ROUNDS):
        h = 1 << (r - 1)
        partners.append((t, dom(x, y + h - 2 * h * ((y // h) % 2), c)))
    x_peer = [(t, dom((x + k) % 4, y, c)) for k in range(1, 4)]
    y_peer = [(t, dom(x, (y + k) % 8, c)) for k in range(1, 8)]
    z_peer = [((t + k) % 8, d) for k in range(1, 8)]

    loads, started, taken = {}, [], set()

    def load(i, s, dst):
        loads[i] = pltpu.make_async_copy(s, dst, ld.at[i])
        loads[i].start()

    load(0, node_h.at[0], table.at[0:256])
    load(1, sblk_h, sblk)
    load(2, src_h, src)
    load(3, rblk_h, rblk)
    load(4, rnode_h, rnode)
    load(5, edge_h.at[0], edge)
    load(6, we_h, we)
    load(7, wr_h, wr)
    load(8, ga_h.at[0], ga)
    load(9, ge_h.at[0], ge)
    load(10, ws_h, ws)
    load(11, wo_h, wo)

    bar = pltpu.get_barrier_semaphore()
    greet = [partners[0]] + y_peer + x_peer + z_peer
    for dev in greet:
        pl.semaphore_signal(bar, inc=1, device_id=dev, device_id_type=MESH)

    def remote(s, dst, ss, rs, dev):
        cp = pltpu.make_async_remote_copy(
            src_ref=s, dst_ref=dst, send_sem=ss, recv_sem=rs, device_id=dev, device_id_type=MESH
        )
        cp.start()
        started.append(cp)
        return cp

    def take(cp):
        cp.wait_recv()
        taken.add(id(cp))

    loads[0].wait()
    loads[1].wait()
    for r in range(ROUNDS):
        pick = jnp.broadcast_to(sblk[:, r : r + 1], (128, 512)) == 0
        lent[r] = jnp.where(pick, table[0:128, :].astype(F32), table[128:256, :].astype(F32)).astype(BF16)
    pl.semaphore_wait(bar, len(greet))
    ex = {}
    for r in (3, 2, 1, 0):
        ex[r] = remote(
            lent.at[r], table.at[256 + 128 * r : 384 + 128 * r], ex_s.at[r], ex_r.at[r], partners[r]
        )

    for i in (2, 3, 4):
        loads[i].wait()
    slots = lax.broadcasted_iota(jnp.int32, (768, 512), 0)
    oht[...] = (slots == src[...]).astype(F32).astype(BF16)
    own = lax.broadcasted_iota(jnp.int32, (256, 128), 0)
    for j in range(4):
        hit = own == rnode[:, 128 * j : 128 * (j + 1)] + rblk[:, j : j + 1] * 128
        rht[:, 128 * j : 128 * (j + 1)] = hit.astype(F32).astype(BF16)
    oh[...] = oht[...].T
    rh[...] = rht[...].T
    for i in (5, 6, 7, 8, 9):
        loads[i].wait()
    for e in (0, 256):
        rows = slice(e, e + 256)
        rrows = mm(rh[rows, :], table[0:256, :]).astype(BF16)
        pre[rows, :] = mm(edge[rows, :], we[...]) + mm(rrows, wr[...])
        gmsg[rows, :] = ge[rows, :].astype(F32) + mm(rh[rows, :], ga[...])
    for i in (10, 11):
        loads[i].wait()

    for r in range(ROUNDS):
        take(ex[r])

    for e in (0, 256):
        rows = slice(e, e + 256)
        sr = mm(oh[rows, :], table[...]).astype(BF16)
        srows[rows, :] = sr
        p = pre[rows, :] + mm(sr, ws[...])
        sig = 1.0 / (1.0 + jnp.exp(-p))
        hv = (p * sig).astype(BF16)
        hid[rows, :] = hv
        dsilu = sig * (1.0 + p * (1.0 - sig))
        proj = mm(hv, wo[...])
        cen = proj - jnp.mean(proj, axis=1, keepdims=True)
        inv = lax.rsqrt(jnp.mean(cen * cen, axis=1, keepdims=True) + 1e-05)
        nrm = cen * inv
        msg[rows, :] = nrm.astype(BF16)
        g = gmsg[rows, :]
        gp = inv * (
            g - jnp.mean(g, axis=1, keepdims=True) - nrm * jnp.mean(g * nrm, axis=1, keepdims=True)
        )
        gp = gp.astype(BF16)
        gproj[rows, :] = gp
        gpre[rows, :] = (mm_nt(gp, wo[...]) * dsilu).astype(BF16)

    core, ret = [], {}
    bufs = ((x_in0, z_in0, mid0), (x_in1, z_in1, mid1), (x_in2, z_in2, mid2))
    first = [[] for _ in CHUNKS]

    def grad(m):
        if m == 0:
            gw = mm_tn(edge[...], gpre[...])
        elif m == 1:
            gw = mm_tn(srows[...], gpre[...])
        elif m == 2:
            gw = mm_tn(table[0:256, :], rsum[...])
        else:
            gw = mm_tn(hid[...], gproj[...])
        gw = gw.reshape(4, 8, 2, 8, 512)
        for xx in range(4):
            for cc in range(2):
                v = gw[xx, :, cc].reshape(64, 512).astype(BF16)
                part[cc, xx, 2 * m] = v[:, 0:256]
                part[cc, xx, 2 * m + 1] = v[:, 256:512]
        core.append(
            remote(
                part.at[1 - c, :, 2 * m : 2 * m + 2],
                core_in.at[:, 2 * m : 2 * m + 2],
                co_s.at[m],
                co_r.at[m],
                partners[0],
            )
        )

    def merge(m):
        take(core[m])
        z2 = slice(2 * m, 2 * m + 2)
        quart[:, z2] = (part[c, :, z2].astype(F32) + core_in[:, z2].astype(F32)).astype(BF16)

    def send_x(i, g):
        _, lo, n = CHUNKS[i]
        zs = slice(4 * g, 4 * g + 4)
        for k in (2, 1, 3):
            first[i].append(
                remote(
                    quart.at[(x + k) % 4, zs, lo : lo + n], bufs[i][0].at[k - 1, zs],
                    xs_s.at[i, g, k - 1], xs_r.at[i, g, k - 1], x_peer[k - 1],
                )
            )

    def send_z(i):
        _, lo, n = CHUNKS[i]
        for k in (4, 3, 5, 2, 6, 1, 7):
            first[i].append(
                remote(
                    quart.at[:, (t + k) % 8, lo : lo + n], bufs[i][1].at[k - 1],
                    zs_s.at[i, k - 1], zs_r.at[i, k - 1], z_peer[k - 1],
                )
            )

    grad(0)
    grad(1)
    rsum[...] = mm(rht[...], gpre[...]).astype(BF16)
    grad(2)
    merge(0)
    merge(1)
    send_x(0, 0)
    grad(3)
    for r in (3, 2, 1, 0):
        rows = slice(256 + 128 * r, 384 + 128 * r)
        slot_out[r] = mm(oht[rows, :], gpre[...]).astype(BF16)
        ret[r] = remote(slot_out.at[r], slot_in.at[r], rt_s.at[r], rt_r.at[r], partners[r])
    merge(2)
    merge(3)
    send_z(1)
    send_x(0, 1)
    send_x(2, 0)
    send_x(2, 1)

    agg_o[0] = mm(rht[...], msg[...]).astype(BF16)
    for e in (0, 256):
        rows = slice(e, e + 256)
        gedge_o[0, rows, :] = (ge[rows, :].astype(F32) + mm_nt(gpre[rows, :], we[...])).astype(BF16)
    own_sum = [mm(oht[128 * b : 128 * (b + 1), :], gpre[...]) for b in range(2)]
    gn_recv = mm_nt(rsum[...], wr[...])

    second = []
    for i, (order, lo, n) in enumerate(CHUNKS):
        xi, zi, mid = bufs[i]
        rs = slice(lo, lo + n)
        for cp in first[i]:
            take(cp)
        sent = []
        if order == "xz":
            acc = quart[x, :, rs].astype(F32)
            for k in range(3):
                acc = acc + xi[k].astype(F32)
            mid[...] = acc.astype(BF16)
            for k in (4, 3, 5, 2, 6, 1, 7):
                sent.append(
                    remote(
                        mid.at[(t + k) % 8], zi.at[k - 1],
                        zs_s.at[i, k - 1], zs_r.at[i, k - 1], z_peer[k - 1],
                    )
                )
        else:
            acc = quart[:, t, rs].astype(F32)
            for k in range(7):
                acc = acc + zi[k].astype(F32)
            mid[...] = acc.astype(BF16)
            for k in (2, 1, 3):
                sent.append(
                    remote(
                        mid.at[(x + k) % 4], xi.at[k - 1],
                        xs_s.at[i, 0, k - 1], xs_r.at[i, 0, k - 1], x_peer[k - 1],
                    )
                )
        second.append(sent)

    for i, (order, lo, n) in enumerate(CHUNKS):
        xi, zi, mid = bufs[i]
        for cp in second[i]:
            take(cp)
        if order == "xz":
            acc = mid[t].astype(F32)
            for k in range(7):
                acc = acc + zi[k].astype(F32)
        else:
            acc = mid[x].astype(F32)
            for k in range(3):
                acc = acc + xi[k].astype(F32)
        for j in range(n // 8):
            sums[lo // 8 + j] = acc[8 * j : 8 * (j + 1), :]

    ysent = []
    for k in (4, 3, 5, 2, 6, 1, 7):
        ysent.append(
            remote(sums.at[(y + k) % 8], y_in.at[k - 1], ys_s.at[k - 1], ys_r.at[k - 1], y_peer[k - 1])
        )

    for r in range(ROUNDS):
        take(ret[r])
        v = slot_in[r].astype(F32)
        for b in range(2):
            own_sum[b] = own_sum[b] + v * (sblk[:, r : r + 1] == b).astype(F32)
    for b in range(2):
        rows = slice(128 * b, 128 * (b + 1))
        gn = gn_recv[rows, :] + mm_nt(own_sum[b].astype(BF16), ws[...])
        gnode_o[0, rows, :] = gn.astype(BF16)

    for cp in ysent:
        take(cp)
    acc = sums[y]
    for k in range(7):
        acc = acc + y_in[k]
    fin[...] = acc
    gsent = []
    for k in (4, 3, 5, 2, 6, 1, 7):
        gsent.append(remote(fin, gath.at[t], ag_s.at[k - 1], ag_r.at[k - 1], z_peer[k - 1]))
    gath[t] = acc
    for cp in gsent:
        take(cp)
    for m in range(4):
        for b in range(2):
            wg_o[m, :, 256 * b : 256 * (b + 1)] = gath[2 * m + b]

    for cp in started:
        cp.wait_send()


def place(*refs):
    copies = [pltpu.make_async_copy(refs[i], refs[i + 4], refs[8].at[i]) for i in range(4)]
    for cp in copies:
        cp.start()
    for cp in copies:
        cp.wait()


def per_device(
    node_lat, edge_lat, grad_edge, grad_agg, weight_edge, weight_send, weight_recv, weight_out,
    edge_src, edge_recv_block, edge_recv_node, send_blocks,
):
    vm, dma = pltpu.VMEM, pltpu.SemaphoreType.DMA
    big = (512, 512)
    scratch = [
        vm((768, 512), BF16), vm(big, BF16), vm(big, BF16), vm((256, 512), BF16),
        vm(big, BF16), vm(big, BF16), vm(big, BF16), vm(big, BF16),
        vm((1, 512), jnp.int32), vm((1, 512), jnp.int32),
        vm((1, 4), jnp.int32), vm((1, 4), jnp.int32),
        vm((4, 128, 512), BF16), vm((512, 768), BF16), vm((768, 512), BF16),
        vm((512, 256), BF16), vm((256, 512), BF16),
        vm(big, F32), vm(big, F32),
        vm(big, BF16), vm(big, BF16), vm(big, BF16), vm(big, BF16), vm(big, BF16),
        vm((4, 128, 512), BF16), vm((4, 128, 512), BF16),
        vm((256, 512), BF16),
        vm((2, 4, 8, 64, 256), BF16), vm((4, 8, 64, 256), BF16), vm((4, 8, 64, 256), BF16),
    ]
    for order, _, n in CHUNKS:
        if order == "xz":
            scratch += [vm((3, 8, n, 256), BF16), vm((7, n, 256), BF16), vm((8, n, 256), BF16)]
        else:
            scratch += [vm((3, n, 256), BF16), vm((7, 4, n, 256), BF16), vm((4, n, 256), BF16)]
    scratch += [
        vm((8, 8, 256), F32), vm((7, 8, 256), F32), vm((8, 256), F32), vm((8, 8, 256), F32),
        dma((12,)), dma((4,)), dma((4,)), dma((4,)), dma((4,)), dma((4,)), dma((4,)),
        dma((3, 2, 3)), dma((3, 2, 3)), dma((3, 7)), dma((3, 7)), dma((7,)), dma((7,)),
        dma((7,)), dma((7,)),
    ]
    hbm = pl.BlockSpec(memory_space=pltpu.HBM)
    vmem = pl.BlockSpec(memory_space=pltpu.VMEM)
    operands = (
        node_lat, edge_lat, grad_edge, grad_agg, weight_edge, weight_send, weight_recv, weight_out,
        edge_src.reshape(1, 512), edge_recv_block.reshape(1, 4),
        edge_recv_node.reshape(1, 512), send_blocks.reshape(1, 4),
    )
    results = pl.pallas_call(
        kernel,
        out_shape=(
            vm((1, 256, 512), BF16), vm((1, 512, 512), BF16), vm((1, 256, 512), BF16), vm((4, 8, 512), F32),
        ),
        in_specs=[hbm] * 12,
        out_specs=(vmem,) * 4,
        scratch_shapes=scratch,
        compiler_params=pltpu.CompilerParams(
            collective_id=0, has_side_effects=True, vmem_limit_bytes=44 << 20
        ),
        name="edge_update_backward",
    )(*(pltpu.with_memory_space_constraint(a, pltpu.HBM) for a in operands))
    return pl.pallas_call(
        place,
        out_shape=tuple(jax.ShapeDtypeStruct(r.shape, r.dtype) for r in results),
        in_specs=[pl.BlockSpec(memory_space=pl.ANY)] * 4,
        out_specs=(hbm,) * 4,
        scratch_shapes=[dma((4,))],
        name="place_results",
    )(*(pltpu.with_memory_space_constraint(r, pltpu.VMEM) for r in results))


def solution(mesh):
    lat = P("traj", "dom", None)
    return jax.shard_map(
        per_device,
        mesh=mesh,
        in_specs=(lat,) * 4 + (P(),) * 4 + (P("dom"),) * 4,
        out_specs=(lat, lat, lat, P(None, "dom", None)),
        check_vma=False,
    )
```

```python
import jax
import jax.numpy as jnp
from jax import lax
from jax.experimental import pallas as pl
from jax.experimental.pallas import tpu as pltpu
from jax.sharding import PartitionSpec as P

ROUNDS = 4
F32 = jnp.float32
BF16 = jnp.bfloat16
MESH = pl.DeviceIdType.MESH
CHUNKS = (("xz", 0, 32), ("zx", 48, 16), ("xz", 32, 16))


def mm(a, b):
    return jnp.dot(a, b, preferred_element_type=F32)


def mm_tn(a, b):
    return lax.dot_general(a, b, (((0,), (0,)), ((), ())), preferred_element_type=F32)


def mm_nt(a, b):
    return lax.dot_general(a, b, (((1,), (1,)), ((), ())), preferred_element_type=F32)


def kernel(
    node_h, edge_h, ge_h, ga_h, we_h, ws_h, wr_h, wo_h, src_h, rblk_h, rnode_h, sblk_h,
    agg_o, gedge_o, gnode_o, wg_o,
    table, edge, ge, ga, we, ws, wr, wo, src, rnode, rblk, sblk,
    lent, oh, oht, rh, rht, pre, gmsg, srows, hid, msg, gproj, gpre, slot_out, slot_in,
    rsum, part, core_in, quart, x_in0, z_in0, mid0, x_in1, z_in1, mid1, x_in2, z_in2, mid2, sums, y_in, fin, gath, edge_t, node_t, early, far0, mrg0, far2, mrg2,
    ld, ex_s, ex_r, rt_s, rt_r, co_s, co_r, xs_s, xs_r, zs_s, zs_r, ys_s, ys_r, ag_s, ag_r,
):
    t = lax.axis_index("traj")
    d = lax.axis_index("dom")
    x, y, c = d // 16, (d // 2) % 8, d % 2

    def dom(xx, yy, cc):
        return xx * 16 + yy * 2 + cc

    partners = [(t, d + 1 - 2 * c)]
    for r in range(1, ROUNDS):
        h = 1 << (r - 1)
        partners.append((t, dom(x, y + h - 2 * h * ((y // h) % 2), c)))
    x_peer = [(t, dom((x + k) % 4, y, c)) for k in range(1, 4)]
    y_peer = [(t, dom(x, (y + k) % 8, c)) for k in range(1, 8)]
    z_peer = [((t + k) % 8, d) for k in range(1, 8)]

    loads, started, taken = {}, [], set()

    def load(i, s, dst):
        loads[i] = pltpu.make_async_copy(s, dst, ld.at[i])
        loads[i].start()

    load(0, node_h.at[0], table.at[0:256])
    load(1, sblk_h, sblk)

    bar = pltpu.get_barrier_semaphore()
    greet = [partners[0]] + y_peer + x_peer + z_peer
    for dev in greet:
        pl.semaphore_signal(bar, inc=1, device_id=dev, device_id_type=MESH)

    def remote(s, dst, ss, rs, dev):
        cp = pltpu.make_async_remote_copy(
            src_ref=s, dst_ref=dst, send_sem=ss, recv_sem=rs, device_id=dev, device_id_type=MESH
        )
        cp.start()
        started.append(cp)
        return cp

    def take(cp):
        cp.wait_recv()
        taken.add(id(cp))

    load(2, src_h, src)
    load(3, rblk_h, rblk)
    load(4, rnode_h, rnode)
    load(5, edge_h.at[0], edge)
    load(6, we_h, we)
    load(7, wr_h, wr)
    load(8, ga_h.at[0], ga)
    load(9, ge_h.at[0], ge)
    load(10, ws_h, ws)
    load(11, wo_h, wo)

    loads[0].wait()
    loads[1].wait()
    pl.semaphore_wait(bar, len(greet))
    ex = {}
    for r in (3, 2, 1, 0):
        pick = jnp.broadcast_to(sblk[:, r : r + 1], (128, 512)) == 0
        lent[r] = jnp.where(pick, table[0:128, :].astype(F32), table[128:256, :].astype(F32)).astype(BF16)
        ex[r] = remote(
            lent.at[r], table.at[256 + 128 * r : 384 + 128 * r], ex_s.at[r], ex_r.at[r], partners[r]
        )

    for i in (2, 3, 4):
        loads[i].wait()
    slots = lax.broadcasted_iota(jnp.int32, (768, 512), 0)
    oht[...] = (slots == src[...]).astype(F32).astype(BF16)
    own = lax.broadcasted_iota(jnp.int32, (256, 128), 0)
    for j in range(4):
        hit = own == rnode[:, 128 * j : 128 * (j + 1)] + rblk[:, j : j + 1] * 128
        rht[:, 128 * j : 128 * (j + 1)] = hit.astype(F32).astype(BF16)
    oh[...] = oht[...].T
    rh[...] = rht[...].T
    for i in (5, 6, 7, 8, 9):
        loads[i].wait()
    for e in (0, 256):
        rows = slice(e, e + 256)
        rrows = mm(rh[rows, :], table[0:256, :]).astype(BF16)
        pre[rows, :] = mm(edge[rows, :], we[...]) + mm(rrows, wr[...])
        gmsg[rows, :] = ge[rows, :].astype(F32) + mm(rh[rows, :], ga[...])
    for i in (10, 11):
        loads[i].wait()
    edge_t[...] = edge[...].T
    node_t[...] = table[0:256, :].T
    take(ex[0])
    take(ex[1])
    for e in (0, 256):
        rows = slice(e, e + 256)
        early[rows, :] = mm(oh[rows, 0:512], table[0:512, :])
    take(ex[2])
    take(ex[3])

    for e in (0, 256):
        rows = slice(e, e + 256)
        sr = (early[rows, :] + mm(oh[rows, 512:768], table[512:768, :])).astype(BF16)
        srows[rows, :] = sr
        p = pre[rows, :] + mm(sr, ws[...])
        sig = 1.0 / (1.0 + jnp.exp(-p))
        hv = (p * sig).astype(BF16)
        hid[rows, :] = hv
        dsilu = sig * (1.0 + p * (1.0 - sig))
        proj = mm(hv, wo[...])
        cen = proj - jnp.mean(proj, axis=1, keepdims=True)
        inv = lax.rsqrt(jnp.mean(cen * cen, axis=1, keepdims=True) + 1e-05)
        nrm = cen * inv
        msg[rows, :] = nrm.astype(BF16)
        g = gmsg[rows, :]
        gp = inv * (
            g - jnp.mean(g, axis=1, keepdims=True) - nrm * jnp.mean(g * nrm, axis=1, keepdims=True)
        )
        gp = gp.astype(BF16)
        gproj[rows, :] = gp
        gpre[rows, :] = (mm_nt(gp, wo[...]) * dsilu).astype(BF16)

    core, ret = [], {}
    bufs = ((x_in0, z_in0, mid0), (x_in1, z_in1, mid1), (x_in2, z_in2, mid2))
    first = [[] for _ in CHUNKS]

    def grad(m):
        if m == 0:
            gw = mm(edge_t[...], gpre[...])
        elif m == 1:
            gw = mm(node_t[...], rsum[...])
        elif m == 2:
            gw = mm_tn(hid[...], gproj[...])
        else:
            gw = mm_tn(srows[...], gpre[...])
        gw = gw.reshape(4, 8, 2, 8, 512)
        for xx in range(4):
            for cc in range(2):
                v = gw[xx, :, cc].reshape(64, 512).astype(BF16)
                part[cc, xx, 2 * m] = v[:, 0:256]
                part[cc, xx, 2 * m + 1] = v[:, 256:512]
        core.append(
            remote(
                part.at[1 - c, :, 2 * m : 2 * m + 2],
                core_in.at[:, 2 * m : 2 * m + 2],
                co_s.at[m],
                co_r.at[m],
                partners[0],
            )
        )

    def merge(m):
        take(core[m])
        z2 = slice(2 * m, 2 * m + 2)
        quart[:, z2] = (part[c, :, z2].astype(F32) + core_in[:, z2].astype(F32)).astype(BF16)

    far, relays = {}, {0: (far0, mrg0), 2: (far2, mrg2)}

    def put_x(i, slot, src, dst, k):
        return remote(src, dst, xs_s.at[i, slot], xs_r.at[i, slot], x_peer[k - 1])

    def send_x(i, g):
        _, lo, n = CHUNKS[i]
        zs, rs = slice(4 * g, 4 * g + 4), slice(lo, lo + n)
        fwd, back = (1, 3) if g == 0 else (3, 1)
        far[i, g] = put_x(i, g, quart.at[(x + 2) % 4, zs, rs], relays[i][0].at[g], fwd)
        first[i].append(
            put_x(i, 2 + g, quart.at[(x + back) % 4, zs, rs], bufs[i][0].at[1 - g, g], back)
        )

    def relay_x(i, g):
        _, lo, n = CHUNKS[i]
        far_in, mrg = relays[i]
        fwd = 1 if g == 0 else 3
        take(far[i, g])
        own = quart[(x + fwd) % 4, 4 * g : 4 * g + 4, lo : lo + n].astype(F32)
        mrg[g] = (own + far_in[g].astype(F32)).astype(BF16)
        first[i].append(put_x(i, 4 + g, mrg.at[g], bufs[i][0].at[g, g], fwd))

    def copy_z(i, k):
        _, lo, n = CHUNKS[i]
        return pltpu.make_async_remote_copy(
            src_ref=quart.at[:, (t + k) % 8, lo : lo + n], dst_ref=bufs[i][1].at[k - 1],
            send_sem=zs_s.at[i, k - 1], recv_sem=zs_r.at[i, k - 1],
            device_id=z_peer[k - 1], device_id_type=MESH,
        )

    def send_z(i, g):
        for k in (4, 3, 5, 2, 6, 1, 7):

            @pl.when(((t + k) % 8) // 4 == g)
            def _(k=k):
                copy_z(i, k).start()

        if g == 1:
            for k in range(1, 8):
                cp = copy_z(i, k)
                started.append(cp)
                first[i].append(cp)

    grad(0)
    rsum[...] = mm(rht[...], gpre[...]).astype(BF16)
    grad(1)
    grad(2)
    merge(0)
    merge(1)
    send_z(1, 0)
    send_x(0, 0)
    send_x(2, 0)
    grad(3)
    merge(2)
    for r in (3, 2, 1, 0):
        rows = slice(256 + 128 * r, 384 + 128 * r)
        slot_out[r] = mm(oht[rows, :], gpre[...]).astype(BF16)
        if r == 2:
            merge(3)
            send_z(1, 1)
            send_x(0, 1)
            send_x(2, 1)
    for r in (3, 2, 1, 0):
        ret[r] = remote(slot_out.at[r], slot_in.at[r], rt_s.at[r], rt_r.at[r], partners[r])

    agg_o[0] = mm(rht[...], msg[...]).astype(BF16)
    relay_x(0, 0)
    relay_x(2, 0)
    for e in (0, 256):
        rows = slice(e, e + 256)
        gedge_o[0, rows, :] = (ge[rows, :].astype(F32) + mm_nt(gpre[rows, :], we[...])).astype(BF16)
    relay_x(0, 1)
    relay_x(2, 1)
    own_sum = [mm(oht[128 * b : 128 * (b + 1), :], gpre[...]) for b in range(2)]
    gn_recv = mm_nt(rsum[...], wr[...])

    second = []
    for i, (order, lo, n) in enumerate(CHUNKS):
        xi, zi, mid = bufs[i]
        rs = slice(lo, lo + n)
        for cp in first[i]:
            take(cp)
        sent = []
        if order == "xz":
            acc = quart[x, :, rs].astype(F32)
            for k in range(2):
                acc = acc + xi[k].astype(F32).reshape(8, n, 256)
            mid[...] = acc.astype(BF16)
            for k in (4, 3, 5, 2, 6, 1, 7):
                sent.append(
                    remote(
                        mid.at[(t + k) % 8], zi.at[k - 1],
                        zs_s.at[i, k - 1], zs_r.at[i, k - 1], z_peer[k - 1],
                    )
                )
        else:
            acc = quart[:, t, rs].astype(F32)
            for k in range(7):
                acc = acc + zi[k].astype(F32)
            mid[...] = acc.astype(BF16)
            for k in (2, 1, 3):
                sent.append(
                    remote(
                        mid.at[(x + k) % 4], xi.at[k - 1],
                        xs_s.at[i, k - 1], xs_r.at[i, k - 1], x_peer[k - 1],
                    )
                )
        second.append(sent)

    for i, (order, lo, n) in enumerate(CHUNKS):
        xi, zi, mid = bufs[i]
        for cp in second[i]:
            take(cp)
        if order == "xz":
            acc = mid[t].astype(F32)
            for k in range(7):
                acc = acc + zi[k].astype(F32)
        else:
            acc = mid[x].astype(F32)
            for k in range(3):
                acc = acc + xi[k].astype(F32)
        for j in range(n // 8):
            sums[lo // 8 + j] = acc[8 * j : 8 * (j + 1), :].astype(BF16)

    ysent = []
    for k in (4, 3, 5, 2, 6, 1, 7):
        ysent.append(
            remote(sums.at[(y + k) % 8], y_in.at[k - 1], ys_s.at[k - 1], ys_r.at[k - 1], y_peer[k - 1])
        )

    for r in range(ROUNDS):
        take(ret[r])
        v = slot_in[r].astype(F32)
        for b in range(2):
            own_sum[b] = own_sum[b] + v * (sblk[:, r : r + 1] == b).astype(F32)
    for b in range(2):
        rows = slice(128 * b, 128 * (b + 1))
        gn = gn_recv[rows, :] + mm_nt(own_sum[b].astype(BF16), ws[...])
        gnode_o[0, rows, :] = gn.astype(BF16)

    for cp in started[:-7]:
        cp.wait_send()
    for cp in ysent:
        take(cp)
    acc = sums[y].astype(F32)
    for k in range(7):
        acc = acc + y_in[k].astype(F32)
    acc = acc.astype(BF16)
    fin[...] = acc
    gsent = []
    for k in (4, 3, 5, 2, 6, 1, 7):
        gsent.append(remote(fin, gath.at[t], ag_s.at[k - 1], ag_r.at[k - 1], z_peer[k - 1]))
    gath[t] = acc
    for cp in gsent:
        take(cp)
    for m in range(4):
        for b in range(2):
            wg_o[(0, 2, 3, 1)[m], :, 256 * b : 256 * (b + 1)] = gath[2 * m + b].astype(F32)

    for cp in ysent + gsent:
        cp.wait_send()


def place(*refs):
    copies = [pltpu.make_async_copy(refs[i], refs[i + 4], refs[8].at[i]) for i in range(4)]
    for cp in copies:
        cp.start()
    for cp in copies:
        cp.wait()


def per_device(
    node_lat, edge_lat, grad_edge, grad_agg, weight_edge, weight_send, weight_recv, weight_out,
    edge_src, edge_recv_block, edge_recv_node, send_blocks,
):
    vm, dma = pltpu.VMEM, pltpu.SemaphoreType.DMA
    big = (512, 512)
    scratch = [
        vm((768, 512), BF16), vm(big, BF16), vm(big, BF16), vm((256, 512), BF16),
        vm(big, BF16), vm(big, BF16), vm(big, BF16), vm(big, BF16),
        vm((1, 512), jnp.int32), vm((1, 512), jnp.int32),
        vm((1, 4), jnp.int32), vm((1, 4), jnp.int32),
        vm((4, 128, 512), BF16), vm((512, 768), BF16), vm((768, 512), BF16),
        vm((512, 256), BF16), vm((256, 512), BF16),
        vm(big, F32), vm(big, F32),
        vm(big, BF16), vm(big, BF16), vm(big, BF16), vm(big, BF16), vm(big, BF16),
        vm((4, 128, 512), BF16), vm((4, 128, 512), BF16),
        vm((256, 512), BF16),
        vm((2, 4, 8, 64, 256), BF16), vm((4, 8, 64, 256), BF16), vm((4, 8, 64, 256), BF16),
    ]
    for order, _, n in CHUNKS:
        if order == "xz":
            scratch += [vm((2, 2, 4, n, 256), BF16), vm((7, n, 256), BF16), vm((8, n, 256), BF16)]
        else:
            scratch += [vm((3, n, 256), BF16), vm((7, 4, n, 256), BF16), vm((4, n, 256), BF16)]
    scratch += [
        vm((8, 8, 256), BF16), vm((7, 8, 256), BF16), vm((8, 256), BF16), vm((8, 8, 256), BF16),
        vm(big, BF16), vm((512, 256), BF16), vm(big, F32),
        *[vm((2, 4, CHUNKS[i][2], 256), BF16) for i in (0, 0, 2, 2)],
        dma((12,)), dma((4,)), dma((4,)), dma((4,)), dma((4,)), dma((4,)), dma((4,)),
        dma((3, 6)), dma((3, 6)), dma((3, 7)), dma((3, 7)), dma((7,)), dma((7,)),
        dma((7,)), dma((7,)),
    ]
    hbm = pl.BlockSpec(memory_space=pltpu.HBM)
    vmem = pl.BlockSpec(memory_space=pltpu.VMEM)
    operands = (
        node_lat, edge_lat, grad_edge, grad_agg, weight_edge, weight_send, weight_recv, weight_out,
        edge_src.reshape(1, 512), edge_recv_block.reshape(1, 4),
        edge_recv_node.reshape(1, 512), send_blocks.reshape(1, 4),
    )
    results = pl.pallas_call(
        kernel,
        out_shape=(
            vm((1, 256, 512), BF16), vm((1, 512, 512), BF16), vm((1, 256, 512), BF16), vm((4, 8, 512), F32),
        ),
        in_specs=[hbm] * 12,
        out_specs=(vmem,) * 4,
        scratch_shapes=scratch,
        compiler_params=pltpu.CompilerParams(
            collective_id=0, has_side_effects=True, vmem_limit_bytes=44 << 20
        ),
        name="edge_update_backward",
    )(*(pltpu.with_memory_space_constraint(a, pltpu.HBM) for a in operands))
    return pl.pallas_call(
        place,
        out_shape=tuple(jax.ShapeDtypeStruct(r.shape, r.dtype) for r in results),
        in_specs=[pl.BlockSpec(memory_space=pl.ANY)] * 4,
        out_specs=(hbm,) * 4,
        scratch_shapes=[dma((4,))],
        name="place_results",
    )(*(pltpu.with_memory_space_constraint(r, pltpu.VMEM) for r in results))


def solution(mesh):
    lat = P("traj", "dom", None)
    return jax.shard_map(
        per_device,
        mesh=mesh,
        in_specs=(lat,) * 4 + (P(),) * 4 + (P("dom"),) * 4,
        out_specs=(lat, lat, lat, P(None, "dom", None)),
        check_vma=False,
    )
```

```python
import jax
import jax.numpy as jnp
from jax import lax
from jax.experimental import pallas as pl
from jax.experimental.pallas import tpu as pltpu
from jax.sharding import PartitionSpec as P

ROUNDS = 4
F32 = jnp.float32
BF16 = jnp.bfloat16
MESH = pl.DeviceIdType.MESH
CHUNKS = (("xz", 0, 32), ("zx", 48, 16), ("xz", 32, 16))


def mm(a, b):
    return jnp.dot(a, b, preferred_element_type=F32)


def mm_tn(a, b):
    return lax.dot_general(a, b, (((0,), (0,)), ((), ())), preferred_element_type=F32)


def mm_nt(a, b):
    return lax.dot_general(a, b, (((1,), (1,)), ((), ())), preferred_element_type=F32)


def kernel(
    node_h, edge_h, ge_h, ga_h, we_h, ws_h, wr_h, wo_h, src_h, rblk_h, rnode_h, sblk_h,
    agg_o, gedge_o, gnode_o, wg_o,
    table, edge, ge, ga, we, ws, wr, wo, src, rnode, rblk, sblk,
    lent, oh, oht, rh, rht, pre, gmsg, srows, hid, msg, gproj, gpre, slot_out, slot_in,
    rsum, part, core_in, quart, x_in0, z_in0, mid0, x_in1, z_in1, mid1, x_in2, z_in2, mid2, sums, y_in, fin, gath, edge_t, node_t, early, far0, mrg0, far2, mrg2,
    ld, ex_s, ex_r, rt_s, rt_r, co_s, co_r, xs_s, xs_r, zs_s, zs_r, ys_s, ys_r, ag_s, ag_r,
):
    t = lax.axis_index("traj")
    d = lax.axis_index("dom")
    x, y, c = d // 16, (d // 2) % 8, d % 2

    def dom(xx, yy, cc):
        return xx * 16 + yy * 2 + cc

    partners = [(t, d + 1 - 2 * c)]
    for r in range(1, ROUNDS):
        h = 1 << (r - 1)
        partners.append((t, dom(x, y + h - 2 * h * ((y // h) % 2), c)))
    x_peer = [(t, dom((x + k) % 4, y, c)) for k in range(1, 4)]
    y_peer = [(t, dom(x, (y + k) % 8, c)) for k in range(1, 8)]
    z_peer = [((t + k) % 8, d) for k in range(1, 8)]

    loads, started, taken = {}, [], set()

    def load(i, s, dst):
        loads[i] = pltpu.make_async_copy(s, dst, ld.at[i])
        loads[i].start()

    load(0, node_h.at[0], table.at[0:256])
    load(1, sblk_h, sblk)

    bar = pltpu.get_barrier_semaphore()
    greet = [partners[0]] + y_peer + x_peer + z_peer
    for dev in greet:
        pl.semaphore_signal(bar, inc=1, device_id=dev, device_id_type=MESH)

    def remote(s, dst, ss, rs, dev):
        cp = pltpu.make_async_remote_copy(
            src_ref=s, dst_ref=dst, send_sem=ss, recv_sem=rs, device_id=dev, device_id_type=MESH
        )
        cp.start()
        started.append(cp)
        return cp

    def take(cp):
        cp.wait_recv()
        taken.add(id(cp))

    loads[0].wait()
    loads[1].wait()
    pl.semaphore_wait(bar, len(greet))
    ex = {}
    for r in (3, 2, 1, 0):
        pick = jnp.broadcast_to(sblk[:, r : r + 1], (128, 512)) == 0
        lent[r] = jnp.where(pick, table[0:128, :].astype(F32), table[128:256, :].astype(F32)).astype(BF16)
        ex[r] = remote(
            lent.at[r], table.at[256 + 128 * r : 384 + 128 * r], ex_s.at[r], ex_r.at[r], partners[r]
        )

    load(2, src_h, src)
    load(3, rblk_h, rblk)
    load(4, rnode_h, rnode)
    load(5, edge_h.at[0], edge)
    load(6, we_h, we)
    load(7, wr_h, wr)
    load(8, ga_h.at[0], ga)
    load(9, ge_h.at[0], ge)
    load(10, ws_h, ws)
    load(11, wo_h, wo)

    for i in (2, 3, 4):
        loads[i].wait()
    slots = lax.broadcasted_iota(jnp.int32, (768, 512), 0)
    oht[...] = (slots == src[...]).astype(F32).astype(BF16)
    own = lax.broadcasted_iota(jnp.int32, (256, 128), 0)
    for j in range(4):
        hit = own == rnode[:, 128 * j : 128 * (j + 1)] + rblk[:, j : j + 1] * 128
        rht[:, 128 * j : 128 * (j + 1)] = hit.astype(F32).astype(BF16)
    oh[...] = oht[...].T
    rh[...] = rht[...].T
    for i in (5, 6, 7, 8, 9):
        loads[i].wait()
    for e in (0, 256):
        rows = slice(e, e + 256)
        rrows = mm(rh[rows, :], table[0:256, :]).astype(BF16)
        pre[rows, :] = mm(edge[rows, :], we[...]) + mm(rrows, wr[...])
        gmsg[rows, :] = ge[rows, :].astype(F32) + mm(rh[rows, :], ga[...])
    for i in (10, 11):
        loads[i].wait()
    edge_t[...] = edge[...].T
    node_t[...] = table[0:256, :].T
    take(ex[0])
    take(ex[1])
    for e in (0, 256):
        rows = slice(e, e + 256)
        early[rows, :] = mm(oh[rows, 0:512], table[0:512, :])
    take(ex[2])
    take(ex[3])

    for e in (0,):
        rows = slice(e, e + 512)
        sr = (early[rows, :] + mm(oh[rows, 512:768], table[512:768, :])).astype(BF16)
        srows[rows, :] = sr
        p = pre[rows, :] + mm(sr, ws[...])
        sig = 1.0 / (1.0 + jnp.exp(-p))
        hv = (p * sig).astype(BF16)
        hid[rows, :] = hv
        dsilu = sig * (1.0 + p * (1.0 - sig))
        proj = mm(hv, wo[...])
        cen = proj - jnp.mean(proj, axis=1, keepdims=True)
        inv = lax.rsqrt(jnp.mean(cen * cen, axis=1, keepdims=True) + 1e-05)
        nrm = cen * inv
        msg[rows, :] = nrm.astype(BF16)
        g = gmsg[rows, :]
        gp = inv * (
            g - jnp.mean(g, axis=1, keepdims=True) - nrm * jnp.mean(g * nrm, axis=1, keepdims=True)
        )
        gp = gp.astype(BF16)
        gproj[rows, :] = gp
        gpre[rows, :] = (mm_nt(gp, wo[...]) * dsilu).astype(BF16)

    core, ret = [], {}
    bufs = ((x_in0, z_in0, mid0), (x_in1, z_in1, mid1), (x_in2, z_in2, mid2))
    first = [[] for _ in CHUNKS]

    def grad(m):
        if m == 0:
            gw = mm(edge_t[...], gpre[...])
        elif m == 1:
            gw = mm(node_t[...], rsum[...])
        elif m == 2:
            gw = mm_tn(hid[...], gproj[...])
        else:
            gw = mm_tn(srows[...], gpre[...])
        gw = gw.reshape(4, 8, 2, 8, 512)
        for xx in range(4):
            for cc in range(2):
                v = gw[xx, :, cc].reshape(64, 512).astype(BF16)
                part[cc, xx, 2 * m] = v[:, 0:256]
                part[cc, xx, 2 * m + 1] = v[:, 256:512]
        core.append(
            remote(
                part.at[1 - c, :, 2 * m : 2 * m + 2],
                core_in.at[:, 2 * m : 2 * m + 2],
                co_s.at[m],
                co_r.at[m],
                partners[0],
            )
        )

    def merge(m):
        take(core[m])
        z2 = slice(2 * m, 2 * m + 2)
        quart[:, z2] = (part[c, :, z2].astype(F32) + core_in[:, z2].astype(F32)).astype(BF16)

    far, relays = {}, {0: (far0, mrg0), 2: (far2, mrg2)}

    def put_x(i, slot, src, dst, k):
        return remote(src, dst, xs_s.at[i, slot], xs_r.at[i, slot], x_peer[k - 1])

    def send_x(i, g):
        _, lo, n = CHUNKS[i]
        zs, rs = slice(4 * g, 4 * g + 4), slice(lo, lo + n)
        fwd, back = (1, 3) if g == 0 else (3, 1)
        far[i, g] = put_x(i, g, quart.at[(x + 2) % 4, zs, rs], relays[i][0].at[g], fwd)
        first[i].append(
            put_x(i, 2 + g, quart.at[(x + back) % 4, zs, rs], bufs[i][0].at[1 - g, g], back)
        )

    def relay_x(i, g):
        _, lo, n = CHUNKS[i]
        far_in, mrg = relays[i]
        fwd = 1 if g == 0 else 3
        take(far[i, g])
        own = quart[(x + fwd) % 4, 4 * g : 4 * g + 4, lo : lo + n].astype(F32)
        mrg[g] = (own + far_in[g].astype(F32)).astype(BF16)
        first[i].append(put_x(i, 4 + g, mrg.at[g], bufs[i][0].at[g, g], fwd))

    def copy_z(i, k):
        _, lo, n = CHUNKS[i]
        return pltpu.make_async_remote_copy(
            src_ref=quart.at[:, (t + k) % 8, lo : lo + n], dst_ref=bufs[i][1].at[k - 1],
            send_sem=zs_s.at[i, k - 1], recv_sem=zs_r.at[i, k - 1],
            device_id=z_peer[k - 1], device_id_type=MESH,
        )

    def send_z(i, g):
        for k in (4, 3, 5, 2, 6, 1, 7):

            @pl.when(((t + k) % 8) // 4 == g)
            def _(k=k):
                copy_z(i, k).start()

        if g == 1:
            for k in range(1, 8):
                cp = copy_z(i, k)
                started.append(cp)
                first[i].append(cp)

    grad(0)
    rsum[...] = mm(rht[...], gpre[...]).astype(BF16)
    grad(1)
    grad(2)
    merge(0)
    merge(1)
    send_z(1, 0)
    send_x(0, 0)
    send_x(2, 0)
    grad(3)
    merge(2)
    for r in (3, 2, 1, 0):
        rows = slice(256 + 128 * r, 384 + 128 * r)
        slot_out[r] = mm(oht[rows, :], gpre[...]).astype(BF16)
        if r == 2:
            merge(3)
            send_z(1, 1)
            send_x(0, 1)
            send_x(2, 1)
    for r in (3, 2, 1, 0):
        ret[r] = remote(slot_out.at[r], slot_in.at[r], rt_s.at[r], rt_r.at[r], partners[r])

    agg_o[0] = mm(rht[...], msg[...]).astype(BF16)
    relay_x(0, 0)
    relay_x(2, 0)
    for e in (0, 256):
        rows = slice(e, e + 256)
        gedge_o[0, rows, :] = (ge[rows, :].astype(F32) + mm_nt(gpre[rows, :], we[...])).astype(BF16)
    relay_x(0, 1)
    relay_x(2, 1)
    own_sum = [mm(oht[128 * b : 128 * (b + 1), :], gpre[...]) for b in range(2)]
    gn_recv = mm_nt(rsum[...], wr[...])

    second = {}
    for i in (0, 2, 1):
        order, lo, n = CHUNKS[i]
        xi, zi, mid = bufs[i]
        rs = slice(lo, lo + n)
        for cp in first[i]:
            take(cp)
        sent = []
        if order == "xz":
            acc = quart[x, :, rs].astype(F32)
            for k in range(2):
                acc = acc + xi[k].astype(F32).reshape(8, n, 256)
            mid[...] = acc.astype(BF16)
            for k in (4, 3, 5, 2, 6, 1, 7):
                sent.append(
                    remote(
                        mid.at[(t + k) % 8], zi.at[k - 1],
                        zs_s.at[i, k - 1], zs_r.at[i, k - 1], z_peer[k - 1],
                    )
                )
        else:
            acc = quart[:, t, rs].astype(F32)
            for k in range(7):
                acc = acc + zi[k].astype(F32)
            mid[...] = acc.astype(BF16)
            for k in (2, 1, 3):
                sent.append(
                    remote(
                        mid.at[(x + k) % 4], xi.at[k - 1],
                        xs_s.at[i, k - 1], xs_r.at[i, k - 1], x_peer[k - 1],
                    )
                )
        second[i] = sent
    settled = [ex[r] for r in range(ROUNDS)] + core + list(far.values())
    for cp in settled + first[0] + first[1] + first[2]:
        cp.wait_send()

    for i in (0, 1, 2):
        order, lo, n = CHUNKS[i]
        xi, zi, mid = bufs[i]
        for cp in second[i]:
            take(cp)
        if order == "xz":
            acc = mid[t].astype(F32)
            for k in range(7):
                acc = acc + zi[k].astype(F32)
        else:
            acc = mid[x].astype(F32)
            for k in range(3):
                acc = acc + xi[k].astype(F32)
        for j in range(n // 8):
            sums[lo // 8 + j] = acc[8 * j : 8 * (j + 1), :].astype(BF16)

    ysent = []
    for k in (4, 3, 5, 2, 6, 1, 7):
        ysent.append(
            remote(sums.at[(y + k) % 8], y_in.at[k - 1], ys_s.at[k - 1], ys_r.at[k - 1], y_peer[k - 1])
        )

    for cp in ysent:
        take(cp)
    acc = sums[y].astype(F32)
    for k in range(7):
        acc = acc + y_in[k].astype(F32)
    acc = acc.astype(BF16)
    fin[...] = acc
    gsent = []
    for k in (4, 3, 5, 2, 6, 1, 7):
        gsent.append(remote(fin, gath.at[t], ag_s.at[k - 1], ag_r.at[k - 1], z_peer[k - 1]))
    gath[t] = acc
    for r in range(ROUNDS):
        take(ret[r])
        v = slot_in[r].astype(F32)
        for b in range(2):
            own_sum[b] = own_sum[b] + v * (sblk[:, r : r + 1] == b).astype(F32)
    for b in range(2):
        rows = slice(128 * b, 128 * (b + 1))
        gn = gn_recv[rows, :] + mm_nt(own_sum[b].astype(BF16), ws[...])
        gnode_o[0, rows, :] = gn.astype(BF16)

    for cp in list(ret.values()) + second[0] + second[1] + second[2]:
        cp.wait_send()
    for cp in gsent:
        take(cp)
    for m in range(4):
        for b in range(2):
            wg_o[(0, 2, 3, 1)[m], :, 256 * b : 256 * (b + 1)] = gath[2 * m + b].astype(F32)

    for cp in ysent + gsent:
        cp.wait_send()


def place(*refs):
    copies = [pltpu.make_async_copy(refs[i], refs[i + 4], refs[8].at[i]) for i in range(4)]
    for cp in copies:
        cp.start()
    for cp in copies:
        cp.wait()


def per_device(
    node_lat, edge_lat, grad_edge, grad_agg, weight_edge, weight_send, weight_recv, weight_out,
    edge_src, edge_recv_block, edge_recv_node, send_blocks,
):
    vm, dma = pltpu.VMEM, pltpu.SemaphoreType.DMA
    big = (512, 512)
    scratch = [
        vm((768, 512), BF16), vm(big, BF16), vm(big, BF16), vm((256, 512), BF16),
        vm(big, BF16), vm(big, BF16), vm(big, BF16), vm(big, BF16),
        vm((1, 512), jnp.int32), vm((1, 512), jnp.int32),
        vm((1, 4), jnp.int32), vm((1, 4), jnp.int32),
        vm((4, 128, 512), BF16), vm((512, 768), BF16), vm((768, 512), BF16),
        vm((512, 256), BF16), vm((256, 512), BF16),
        vm(big, F32), vm(big, F32),
        vm(big, BF16), vm(big, BF16), vm(big, BF16), vm(big, BF16), vm(big, BF16),
        vm((4, 128, 512), BF16), vm((4, 128, 512), BF16),
        vm((256, 512), BF16),
        vm((2, 4, 8, 64, 256), BF16), vm((4, 8, 64, 256), BF16), vm((4, 8, 64, 256), BF16),
    ]
    for order, _, n in CHUNKS:
        if order == "xz":
            scratch += [vm((2, 2, 4, n, 256), BF16), vm((7, n, 256), BF16), vm((8, n, 256), BF16)]
        else:
            scratch += [vm((3, n, 256), BF16), vm((7, 4, n, 256), BF16), vm((4, n, 256), BF16)]
    scratch += [
        vm((8, 8, 256), BF16), vm((7, 8, 256), BF16), vm((8, 256), BF16), vm((8, 8, 256), BF16),
        vm(big, BF16), vm((512, 256), BF16), vm(big, F32),
        *[vm((2, 4, CHUNKS[i][2], 256), BF16) for i in (0, 0, 2, 2)],
        dma((12,)), dma((4,)), dma((4,)), dma((4,)), dma((4,)), dma((4,)), dma((4,)),
        dma((3, 6)), dma((3, 6)), dma((3, 7)), dma((3, 7)), dma((7,)), dma((7,)),
        dma((7,)), dma((7,)),
    ]
    hbm = pl.BlockSpec(memory_space=pltpu.HBM)
    vmem = pl.BlockSpec(memory_space=pltpu.VMEM)
    operands = (
        node_lat, edge_lat, grad_edge, grad_agg, weight_edge, weight_send, weight_recv, weight_out,
        edge_src.reshape(1, 512), edge_recv_block.reshape(1, 4),
        edge_recv_node.reshape(1, 512), send_blocks.reshape(1, 4),
    )
    results = pl.pallas_call(
        kernel,
        out_shape=(
            vm((1, 256, 512), BF16), vm((1, 512, 512), BF16), vm((1, 256, 512), BF16), vm((4, 8, 512), F32),
        ),
        in_specs=[hbm] * 12,
        out_specs=(vmem,) * 4,
        scratch_shapes=scratch,
        compiler_params=pltpu.CompilerParams(
            collective_id=0, has_side_effects=True, vmem_limit_bytes=44 << 20
        ),
        name="edge_update_backward",
    )(*(pltpu.with_memory_space_constraint(a, pltpu.HBM) for a in operands))
    return pl.pallas_call(
        place,
        out_shape=tuple(jax.ShapeDtypeStruct(r.shape, r.dtype) for r in results),
        in_specs=[pl.BlockSpec(memory_space=pl.ANY)] * 4,
        out_specs=(hbm,) * 4,
        scratch_shapes=[dma((4,))],
        name="place_results",
    )(*(pltpu.with_memory_space_constraint(r, pltpu.VMEM) for r in results))


def solution(mesh):
    lat = P("traj", "dom", None)
    return jax.shard_map(
        per_device,
        mesh=mesh,
        in_specs=(lat,) * 4 + (P(),) * 4 + (P("dom"),) * 4,
        out_specs=(lat, lat, lat, P(None, "dom", None)),
        check_vma=False,
    )
```
